512 devices in a mesh: depth: 32 (over z_hi, y, core), strip: 4 (over z_lo), freq: 4 (over x).
Axes of the slice: x: 4, y: 4, z: 16 (z_hi: 4, z_lo: 4; z = z_hi * 4 + z_lo), core: 2. Of those that a mesh axis runs over, the one named last changes fastest.
Arguments:
- down_state: float32 [64, 2, 8, 32, 1024], P('depth', None, 'freq', 'strip'), may hold values from -6 to 6
- up_state: float32 [64, 2, 8, 32, 1024], P('depth', None, 'freq', 'strip'), may hold values from -6 to 6
- reflect: float32 [64, 32, 1024], P('depth', 'strip'), may hold values from -3 to 3
- layer_mask: int32 [64, 32, 1024], P('depth', 'strip'), may hold values 0 or 1
- classes: int32 [64, 32, 1024], P('depth', 'strip'), may hold values from 0 to 63
- coeffs: float32 [64, 2, 8, 8], P(None, None, 'freq'), may hold values from -1.2 to 1.2
Outputs:
- down_out: float32 [64, 2, 8, 32, 1024], P('depth', None, 'freq', 'strip')
- up_out: float32 [64, 2, 8, 32, 1024], P('depth', None, 'freq', 'strip')
- image: float32 [64, 32, 1024], P('depth', 'strip', 'freq')
The draws below stay inside these ranges and needn't reach their ends.
All inputs are finite; a program needn't handle non-finite values. No bound on the sum of `layer_mask` on one device may be relied on, other than what follows from the above.
Results may differ from the reference program's by a relative error of at most 0.0003.
Values sent between devices are 32-bit elements; how exact they have to be, the bound alone decides.
No kernel may reach another device: no remote copies, remote signals or barrier semaphores. Data moves between devices by JAX's collectives and lax.ppermute only.
A program may use at most 64 MiB of HBM per device.

```python
import jax
import jax.numpy as jnp
from jax import lax

NY = 1024
DZ = 2
TICKS = 2
TERMS = 8
CLASSES = 64
NX = 32
FREQS = 8
NZ = 64


def touch_ends(values, rng, smallest, high):
    dims = values.shape
    spot = [jax.random.randint(jax.random.fold_in(rng, axis), (), 0, dims[axis]) for axis in range(len(dims))]
    values = values.at[tuple(spot)].set(smallest)
    longest = dims.index(max(dims))
    spot[longest] = (spot[longest] + 1) % dims[longest]
    return values.at[tuple(spot)].set(high)


def block_scale(stream_key, extent, pieces, low, top_value):
    factor_of, own = 1.0, jax.random.fold_in(stream_key, 6)
    for position, parts in pieces:
        steps = jnp.exp(jax.random.uniform(jax.random.fold_in(own, position), (parts,), jnp.float32, low / len(pieces), top_value / len(pieces)))
        factor_of = factor_of * jnp.repeat(steps, extent[position] // parts).reshape([-1 if axis == position else 1 for axis in range(len(extent))])
    return factor_of


def bell_draw(stream_key, extent, width, limit, pieces=(), kind=jnp.bfloat16):
    factor_of = block_scale(stream_key, extent, pieces, -0.22, 0.18) if pieces else 1.0
    values = jax.random.normal(stream_key, extent, jnp.float32) * width * factor_of
    return jnp.minimum(jnp.maximum(values, -limit), limit).astype(kind)


def setup_inputs(seed: int = 0) -> dict:
    arg_keys = jax.random.split(jax.random.key(seed), 7)
    return {
        "down_state": bell_draw(arg_keys[0], (NZ, 2, FREQS, NX, NY), 1.0, 6.0, ((0, 32), (2, 4), (3, 4)), jnp.float32),
        "up_state": bell_draw(arg_keys[1], (NZ, 2, FREQS, NX, NY), 1.0, 6.0, ((0, 32), (2, 4), (3, 4)), jnp.float32),
        "reflect": bell_draw(arg_keys[2], (NZ, NX, NY), 0.5, 3.0, ((0, 32), (1, 4)), jnp.float32),
        "layer_mask": touch_ends((jax.random.randint(arg_keys[3], (NZ, NX, NY), 0, 4) < 3).astype(jnp.int32), jax.random.fold_in(arg_keys[3], 1), 0, 1),
        "classes": touch_ends(jax.random.randint(arg_keys[4], (NZ, NX, NY), 0, CLASSES), jax.random.fold_in(arg_keys[4], 1), 0, CLASSES - 1).astype(jnp.int32),
        "coeffs": bell_draw(arg_keys[5], (CLASSES, 2, FREQS, TERMS), 0.2, 1.2, ((2, 4),), jnp.float32),
    }


def lateral(wavefield):
    padded = jnp.pad(wavefield, ((0, 0), (0, 0), (1, 1), (1, 1)))
    return ((padded[:, :, 2:, 1:-1] + padded[:, :, :-2, 1:-1]) + (padded[:, :, 1:-1, 2:] + padded[:, :, 1:-1, :-2])) * 0.25


def apply_filter(wavefield, table):
    terms = [wavefield, lateral(wavefield)]
    for order in range(2, TERMS):
        terms.append(2.0 * lateral(terms[-1]) - terms[-2])
    real_sum = table[0, :, 0] * terms[0][0] - table[1, :, 0] * terms[0][1]
    imag_sum = table[0, :, 0] * terms[0][1] + table[1, :, 0] * terms[0][0]
    for order in range(1, TERMS):
        real_sum = real_sum + (table[0, :, order] * terms[order][0] - table[1, :, order] * terms[order][1])
        imag_sum = imag_sum + (table[0, :, order] * terms[order][1] + table[1, :, order] * terms[order][0])
    return jnp.stack([real_sum, imag_sum])


def sweep(old_self, old_other, coupling, classes, coeffs, downward):
    levels = jnp.arange(NZ, dtype=jnp.int32)
    zeros = jnp.zeros_like(old_self[:1])
    if downward:
        entering = jnp.concatenate([zeros, old_self[:-1]], 0)
        border = 0
    else:
        entering = jnp.concatenate([old_self[1:], zeros], 0)
        border = DZ - 1

    def step(running, inputs):
        level, entry_old, other, rate, cls = inputs
        start = jnp.where(level % DZ == border, entry_old, running)
        table = jnp.transpose(coeffs[cls], (2, 3, 4, 0, 1))
        result = apply_filter(start + rate[None, None] * other, table)
        return result, result

    _, result = lax.scan(step, jnp.zeros_like(old_self[0]), (levels, entering, old_other, coupling, classes), reverse=not downward)
    return result


def reference(down_state, up_state, reflect, layer_mask, classes, coeffs):
    coupling = reflect * layer_mask.astype(jnp.float32)
    down = down_state
    upward = up_state
    for tick in range(TICKS):
        new_down = sweep(down, upward, coupling, classes, coeffs, True)
        new_up = sweep(upward, down, coupling, classes, coeffs, False)
        down, upward = new_down, new_up
    correlation = jnp.sum(down[:, 0] * upward[:, 0] + down[:, 1] * upward[:, 1], axis=1)
    illumination = jnp.sum(down[:, 0] * down[:, 0] + down[:, 1] * down[:, 1], axis=1)
    image = correlation / (1.0 + illumination)
    return down, upward, image
```

```python
import jax
import jax.numpy as jnp
from jax import lax
from jax.experimental import pallas as pl
from jax.experimental.pallas import tpu as pltpu
from jax.sharding import PartitionSpec as P

TICKS = 2
TERMS = 8
CLASSES = 64
LANES = 128
ROWS = 8
WIDE = 5
HALF = 4
FOLD = 4
TILE = (ROWS, LANES)
FIELD = (2, WIDE, FOLD) + TILE

VM = pl.BlockSpec(memory_space=pltpu.VMEM)
SM = pl.BlockSpec(memory_space=pltpu.SMEM)


def call(body, outs, scratch, limit, *args):
    many = isinstance(outs, (list, tuple)) and isinstance(outs[0], (list, tuple))
    shapes = [jax.ShapeDtypeStruct(s, jnp.float32) for s in outs] if many else jax.ShapeDtypeStruct(outs, jnp.float32)
    return pl.pallas_call(
        body,
        out_shape=shapes,
        in_specs=[SM if a.dtype == jnp.int32 and a.ndim == 1 else VM for a in args],
        out_specs=[VM] * len(outs) if many else VM,
        scratch_shapes=[pltpu.VMEM(s, jnp.float32) for s in scratch],
        compiler_params=pltpu.CompilerParams(vmem_limit_bytes=limit),
    )(*args)


def columns(tile):
    return slice(tile * LANES, (tile + 1) * LANES)


def pack_kernel(info, down, up, reflect, mask, classes, from_core, from_far, send):
    even = info[0] == 0
    for tile in range(2 * HALF):
        at = columns(tile)
        c = [reflect[lv, :, at] * mask[lv, :, at].astype(jnp.float32) for lv in range(2)]
        cls = [classes[lv, :, at].astype(jnp.float32) for lv in range(2)]
        places = [(h, tile - 3 * h) for h in range(2) if 0 <= tile - 3 * h < WIDE]
        for f in range(2):
            values = []
            for r in range(2):
                other = up if r == 0 else down
                for p in range(2):
                    a, b = from_core[p, f, :, at], from_far[p, f, :, at]
                    entry = jnp.where(even, b, a) if r == 0 else jnp.where(even, a, b)
                    values.append(entry + c[r] * other[r, p, f, :, at])
                for p in range(2):
                    values.append(c[1 - r] * other[1 - r, p, f, :, at])
            values += c + cls
            for h, j in places:
                for v, value in enumerate(values):
                    send[2 * h + f, v, j] = value


def filtered(read, write, level, table, terms, total):
    lane = lax.broadcasted_iota(jnp.int32, TILE, 1)
    sub = lax.broadcasted_iota(jnp.int32, TILE, 0)
    first_lane, last_lane = lane == 0, lane == LANES - 1
    first_sub, last_sub = sub == 0, sub == ROWS - 1
    spots = [(i, j) for i in range(FOLD) for j in range(WIDE)]

    def gather(order, i, j, real, imag):
        cr, ci = table[level, order, 0, j, i], table[level, order, 1, j, i]
        return cr * real - ci * imag, cr * imag + ci * real

    for i, j in spots:
        real, imag = read(0, j, i), read(1, j, i)
        terms[0, 0, j, i], terms[0, 1, j, i] = real, imag
        total[0, j, i], total[1, j, i] = gather(0, i, j, real, imag)
    for order in range(1, TERMS):
        now, before, new = (order - 1) % 3, (order - 2) % 3, order % 3
        for i in range(FOLD):
            made = []
            for p in range(2):
                here = [terms[now, p, j, i] for j in range(WIDE)]
                ahead = [pltpu.roll(x, 1, 1) for x in here]
                behind = [pltpu.roll(x, LANES - 1, 1) for x in here]
                row = []
                for j in range(WIDE):
                    west = jnp.where(first_lane, ahead[j - 1] if j else 0.0, ahead[j])
                    east = jnp.where(last_lane, behind[j + 1] if j + 1 < WIDE else 0.0, behind[j])
                    if i:
                        north = terms[now, p, j, i - 1]
                    else:
                        north = jnp.where(first_sub, 0.0, pltpu.roll(terms[now, p, j, FOLD - 1], 1, 0))
                    if i + 1 < FOLD:
                        south = terms[now, p, j, i + 1]
                    else:
                        south = jnp.where(last_sub, 0.0, pltpu.roll(terms[now, p, j, 0], ROWS - 1, 0))
                    around = (south + north) + (east + west)
                    if order == 1:
                        term = around * 0.25
                    else:
                        term = around * 0.5 - terms[before, p, j, i]
                    row.append(term)
                    if order + 1 < TERMS:
                        terms[new, p, j, i] = term
                made.append(row)
            for j in range(WIDE):
                dr, di = gather(order, i, j, made[0][j], made[1][j])
                real, imag = total[0, j, i] + dr, total[1, j, i] + di
                if order + 1 < TERMS:
                    total[0, j, i], total[1, j, i] = real, imag
                else:
                    write(0, j, i, real)
                    write(1, j, i, imag)


def first_kernel(info, recv, coeffs, state, to_core, to_far, coupling, table, rows, terms, total):
    f = info[1]
    for v in range(12):
        for j in range(WIDE):
            for s in range(FOLD):
                rows[v, j, s * ROWS : (s + 1) * ROWS, :] = recv[s, v, j]

    def folded(v, j, i):
        return rows[v, j, pl.ds(i, ROWS, stride=FOLD), :]

    for lv in range(2):
        for j in range(WIDE):
            for i in range(FOLD):
                coupling[lv, j, i] = folded(8 + lv, j, i)

    def build(order, carry):
        for p in range(2):
            lookup = jnp.broadcast_to(coeffs[f, p, pl.ds(order, 1), :], TILE)
            for lv in range(2):
                for j in range(WIDE):
                    for i in range(FOLD):
                        cls = folded(10 + lv, j, i).astype(jnp.int32)
                        table[lv, order, p, j, i] = jnp.take_along_axis(lookup, cls, axis=1, mode="promise_in_bounds")
        return carry

    lax.fori_loop(0, TERMS, build, 0)

    def sweep(r, carry):
        start, end = r, 1 - r

        def write_start(p, j, i, x):
            state[r, start, p, j, i] = x

        def write_end(p, j, i, x):
            state[r, end, p, j, i] = x

        filtered(lambda p, j, i: folded(4 * r + p, j, i), write_start, start, table, terms, total)
        filtered(
            lambda p, j, i: state[r, start, p, j, i] + folded(4 * r + 2 + p, j, i),
            write_end, end, table, terms, total,
        )
        return carry

    lax.fori_loop(0, 2, sweep, 0)
    even = info[0] == 0

    @pl.when(even)
    def _():
        to_core[...] = state[0, 1]
        to_far[...] = state[1, 0]

    @pl.when(jnp.logical_not(even))
    def _():
        to_core[...] = state[1, 0]
        to_far[...] = state[0, 1]


def second_kernel(info, from_core, from_far, state, coupling, table, send, result, rows, terms, total):
    parity, h = info[0], info[2]

    def sweep(r, carry):
        start, end = r, 1 - r
        core = parity + r == 1

        def read_start(p, j, i):
            entry = jnp.where(core, from_core[p, j, i], from_far[p, j, i])
            return entry + coupling[start, j, i] * state[1 - r, start, p, j, i]

        def read_end(p, j, i):
            return result[p, j, i] + coupling[end, j, i] * state[1 - r, end, p, j, i]

        def write(p, j, i, x):
            result[p, j, i] = x
            rows[p, j, pl.ds(i, ROWS, stride=FOLD), :] = x

        def put(level):
            for p in range(2):
                for j in range(HALF):
                    for s in range(FOLD):
                        send[s, 2 * r + level, p, j] = rows[p, h + j, s * ROWS : (s + 1) * ROWS, :]

        filtered(read_start, write, start, table, terms, total)
        put(start)
        filtered(read_end, write, end, table, terms, total)
        put(end)
        return carry

    lax.fori_loop(0, 2, sweep, 0)


def unpack_kernel(recv, down, up, sums):
    for lv in range(2):
        for h in range(2):
            for j in range(HALF):
                tile = HALF * h + j
                at = columns(tile)
                corr = illum = None
                for f in range(2):
                    s = 2 * h + f
                    d = [recv[s, lv, p, j] for p in range(2)]
                    u = [recv[s, 2 + lv, p, j] for p in range(2)]
                    for p in range(2):
                        down[lv, p, f, :, at] = d[p]
                        up[lv, p, f, :, at] = u[p]
                    one, two = d[0] * u[0] + d[1] * u[1], d[0] * d[0] + d[1] * d[1]
                    corr = one if corr is None else corr + one
                    illum = two if illum is None else illum + two
                sums[tile // 2, 0, lv, tile % 2] = corr
                sums[tile // 2, 1, lv, tile % 2] = illum


def image_kernel(recv, image):
    for lv in range(2):
        for t in range(2):
            corr = (recv[0, 0, lv, t] + recv[1, 0, lv, t]) + (recv[2, 0, lv, t] + recv[3, 0, lv, t])
            illum = (recv[0, 1, lv, t] + recv[1, 1, lv, t]) + (recv[2, 1, lv, t] + recv[3, 1, lv, t])
            image[lv, :, columns(t)] = corr / (1.0 + illum)


def local(down_state, up_state, reflect, layer_mask, classes, coeffs):
    depths = lax.axis_size("depth")
    position = lax.axis_index("depth")
    strip = lax.axis_index("strip")
    even = position % 2 == 0
    info = jnp.stack([position % 2, strip % 2, strip // 2]).astype(jnp.int32)
    pairs = [(i, i ^ 1) for i in range(depths)]
    far = [q for i in range(1, depths - 1, 2) for q in ((i, i + 1), (i + 1, i))]

    def crossed(to_core, to_far):
        return lax.ppermute(to_core, "depth", pairs), lax.ppermute(to_far, "depth", far)

    lookup = jnp.pad(jnp.transpose(coeffs, (2, 1, 3, 0)), ((0, 0), (0, 0), (0, 0), (0, LANES - CLASSES)))
    low, high = down_state[1], up_state[0]
    from_core, from_far = crossed(jnp.where(even, low, high), jnp.where(even, high, low))
    send = call(
        pack_kernel, (FOLD, 12, WIDE) + TILE, [], 16 << 20,
        info, down_state, up_state, reflect, layer_mask, classes, from_core, from_far,
    )
    recv = lax.all_to_all(send, "strip", 0, 0)
    work = [(3,) + FIELD, FIELD]
    state, to_core, to_far, coupling, table = call(
        first_kernel,
        [(2, 2) + FIELD, FIELD, FIELD, (2, WIDE, FOLD) + TILE, (2, TERMS) + FIELD],
        [(12, WIDE, FOLD * ROWS, LANES)] + work, 24 << 20,
        info, recv, lookup,
    )
    from_core, from_far = crossed(to_core, to_far)
    send = call(
        second_kernel, (FOLD, 4, 2, HALF) + TILE,
        [FIELD, (2, WIDE, FOLD * ROWS, LANES)] + work, 24 << 20,
        info, from_core, from_far, state, coupling, table,
    )
    recv = lax.all_to_all(send, "strip", 0, 0)
    whole = down_state.shape
    down, up, sums = call(unpack_kernel, [whole, whole, (4, 2, 2, 2) + TILE], [], 16 << 20, recv)
    sums = lax.all_to_all(sums, "freq", 0, 0)
    image = call(image_kernel, (2, ROWS, 2 * LANES), [], 4 << 20, sums)
    return down, up, image


def solution(mesh):
    placed = (
        P("depth", None, "freq", "strip", None),
        P("depth", None, "freq", "strip", None),
        P("depth", "strip", None),
        P("depth", "strip", None),
        P("depth", "strip", None),
        P(None, None, "freq", None),
    )
    return jax.shard_map(
        local,
        mesh=mesh,
        in_specs=placed,
        out_specs=(
            P("depth", None, "freq", "strip", None),
            P("depth", None, "freq", "strip", None),
            P("depth", "strip", "freq"),
        ),
        check_vma=False,
    )
```

```python
import functools

import jax
import jax.numpy as jnp
from jax import lax
from jax.experimental import pallas as pl
from jax.experimental.pallas import tpu as pltpu
from jax.sharding import PartitionSpec as P


TERMS = 8
CLASSES = 64
LANES = 128
ROWS = 8
WIDE = 5
HALF = 4
FOLD = 4
VALUES = 12
EDGE = 32
PACK = LANES // EDGE
TILE = (ROWS, LANES)
FIELD = (2, WIDE, FOLD) + TILE

VM = pl.BlockSpec(memory_space=pltpu.VMEM)
SM = pl.BlockSpec(memory_space=pltpu.SMEM)
HB = pl.BlockSpec(memory_space=pltpu.HBM)


def call(body, outs, scratch, limit, *args, stay=0):
    many = isinstance(outs, (list, tuple)) and isinstance(outs[0], (list, tuple))
    shapes = [jax.ShapeDtypeStruct(s, jnp.float32) for s in outs] if many else jax.ShapeDtypeStruct(outs, jnp.float32)
    specs = [SM if n == 0 and a.dtype == jnp.int32 else HB if 1 <= n <= stay else VM for n, a in enumerate(args)]
    return pl.pallas_call(
        body,
        out_shape=shapes,
        in_specs=specs,
        out_specs=[VM] * len(outs) if many else VM,
        scratch_shapes=[pltpu.VMEM(s, jnp.float32) if isinstance(s, tuple) else s for s in scratch],
        compiler_params=pltpu.CompilerParams(vmem_limit_bytes=limit),
    )(*args)


def columns(tile):
    return slice(tile * LANES, (tile + 1) * LANES)


def pack_kernel(info, *refs):
    _, _, _, _, _, send, fields, reflects, masks, cells, sems = refs
    held = (fields.at[0], fields.at[1], reflects, masks, cells)
    copies = [pltpu.make_async_copy(a, b, sems.at[n]) for n, (a, b) in enumerate(zip(refs[:5], held))]
    for copy in copies:
        copy.start()
    for copy in copies:
        copy.wait()
    parity = info[0]
    lane = lax.broadcasted_iota(jnp.int32, TILE, 1)
    for tile in range(2 * HALF):
        at = columns(tile)
        shared = [reflects[lv, :, at] * masks[lv, :, at].astype(jnp.float32) for lv in range(2)]
        shared += [cells[lv, :, at].astype(jnp.float32) for lv in range(2)]
        h = tile // HALF
        for f in range(2):
            values = []
            for r in (1 - parity, parity):
                for level in (1 - r, r):
                    values += [fields[r, level, p, f, :, at] for p in range(2)]
            values += shared
            for v, value in enumerate(values):
                send[2 * h + f, HALF * v + tile % HALF] = value
            if tile in (HALF - 1, HALF):
                other = 1 - h
                from_lane = 0 if tile == HALF else LANES - EDGE
                for group in range(VALUES // PACK):
                    packed = None
                    for q in range(PACK):
                        shift = (EDGE * q - from_lane) % LANES
                        moved = values[PACK * group + q]
                        moved = pltpu.roll(moved, shift, 1) if shift else moved
                        packed = moved if packed is None else jnp.where(lane >= EDGE * q, moved, packed)
                    send[2 * other + f, HALF * VALUES + group] = packed


def fold_kernel(info, recv, first_end, first_start, second_end, second_start, coupling, cells, rows):
    h = info[2]
    lane = lax.broadcasted_iota(jnp.int32, TILE, 1)
    inside = jnp.where(h == 0, lane, LANES - 1 - lane) < EDGE
    for s in range(FOLD):
        at = slice(s * ROWS, (s + 1) * ROWS)
        for v in range(VALUES):
            for j in range(HALF):
                rows[v, h + j, at, :] = recv[s, HALF * v + j]
            packed = recv[s, HALF * VALUES + v // PACK]
            moved = pltpu.roll(packed, (LANES - EDGE * (v % PACK)) % LANES + (LANES - EDGE) * h, 1)
            rows[v, HALF * (1 - h), at, :] = jnp.where(inside, moved, 0.0)

    def folded(v, j, i):
        return rows[v, j, pl.ds(i, ROWS, stride=FOLD), :]

    for j in range(WIDE):
        for i in range(FOLD):
            for p in range(2):
                first_end[p, j, i] = folded(p, j, i)
                first_start[p, j, i] = folded(2 + p, j, i)
                second_end[p, j, i] = folded(4 + p, j, i)
                second_start[p, j, i] = folded(6 + p, j, i)
            for lv in range(2):
                coupling[lv, j, i] = folded(8 + lv, j, i)
                cells[lv, j, i] = folded(10 + lv, j, i)


def table_kernel(info, cells, coeffs, table):
    f = info[1]

    def build(order, carry):
        lookups = [jnp.broadcast_to(coeffs[f, p, pl.ds(order, 1), :], TILE) for p in range(2)]
        for lv in range(2):
            for j in range(WIDE):
                for i in range(FOLD):
                    cls = cells[lv, j, i].astype(jnp.int32)
                    for p in range(2):
                        table[lv, order, p, j, i] = jnp.take_along_axis(
                            lookups[p], cls, axis=1, mode="promise_in_bounds"
                        )
        return carry

    lax.fori_loop(0, TERMS, build, 0)


def filtered(read, write, level, table, terms, total):
    lane = lax.broadcasted_iota(jnp.int32, TILE, 1)
    sub = lax.broadcasted_iota(jnp.int32, TILE, 0)
    first_lane, last_lane = lane == 0, lane == LANES - 1
    first_sub, last_sub = sub == 0, sub == ROWS - 1
    spots = [(i, j) for i in range(FOLD) for j in range(WIDE)]

    def gather(order, i, j, real, imag):
        cr, ci = table[level, order, 0, j, i], table[level, order, 1, j, i]
        return cr * real - ci * imag, cr * imag + ci * real

    for i, j in spots:
        real, imag = read(0, j, i), read(1, j, i)
        terms[0, 0, j, i], terms[0, 1, j, i] = real, imag
        total[0, j, i], total[1, j, i] = gather(0, i, j, real, imag)
    for order in range(1, TERMS):
        now, before, new = (order - 1) % 3, (order - 2) % 3, order % 3
        for i in range(FOLD):
            made = []
            for p in range(2):
                here = [terms[now, p, j, i] for j in range(WIDE)]
                ahead = [pltpu.roll(x, 1, 1) for x in here]
                behind = [pltpu.roll(x, LANES - 1, 1) for x in here]
                row = []
                for j in range(WIDE):
                    west = jnp.where(first_lane, ahead[j - 1] if j else 0.0, ahead[j])
                    east = jnp.where(last_lane, behind[j + 1] if j + 1 < WIDE else 0.0, behind[j])
                    if i:
                        north = terms[now, p, j, i - 1]
                    else:
                        north = jnp.where(first_sub, 0.0, pltpu.roll(terms[now, p, j, FOLD - 1], 1, 0))
                    if i + 1 < FOLD:
                        south = terms[now, p, j, i + 1]
                    else:
                        south = jnp.where(last_sub, 0.0, pltpu.roll(terms[now, p, j, 0], ROWS - 1, 0))
                    around = (south + north) + (east + west)
                    if order == 1:
                        term = around * 0.25
                    else:
                        term = around * 0.5 - terms[before, p, j, i]
                    row.append(term)
                    if order + 1 < TERMS:
                        terms[new, p, j, i] = term
                made.append(row)
            for j in range(WIDE):
                dr, di = gather(order, i, j, made[0][j], made[1][j])
                real, imag = total[0, j, i] + dr, total[1, j, i] + di
                if order + 1 < TERMS:
                    total[0, j, i], total[1, j, i] = real, imag
                else:
                    write(0, j, i, real)
                    write(1, j, i, imag)


def direction(info, second):
    return info[0] if second else 1 - info[0]


def first_kernel(second, info, entry, start_other, end_other, coupling, table, *refs):
    start_out, end_out, terms, total = refs[-4:]
    r = direction(info, second)
    start, end = r, 1 - r

    def read_start(p, j, i):
        return entry[p, j, i] + coupling[start, j, i] * end_other[p, j, i]

    def read_end(p, j, i):
        return start_out[p, j, i] + coupling[end, j, i] * start_other[p, j, i]

    def write_start(p, j, i, x):
        start_out[p, j, i] = x

    def write_end(p, j, i, x):
        end_out[p, j, i] = x

    filtered(read_start, write_start, start, table, terms, total)
    filtered(read_end, write_end, end, table, terms, total)


def second_kernel(second, info, entry, start_other, end_other, coupling, table, *refs):
    if second:
        earlier, send, result, rows, terms, total = refs
    else:
        send, result, rows, terms, total = refs
    r, h = direction(info, second), info[2]
    start, end = r, 1 - r

    def read_start(p, j, i):
        return entry[p, j, i] + coupling[start, j, i] * end_other[p, j, i]

    def read_end(p, j, i):
        return result[p, j, i] + coupling[end, j, i] * start_other[p, j, i]

    def write(p, j, i, x):
        result[p, j, i] = x
        rows[p, j, pl.ds(i, ROWS, stride=FOLD), :] = x

    def put(level):
        for p in range(2):
            for j in range(HALF):
                for s in range(FOLD):
                    value = rows[p, h + j, s * ROWS : (s + 1) * ROWS, :]
                    if second:
                        send[s, 2 * r + level, p, j] = value
                    else:
                        send[s, level, p, j] = value

    filtered(read_start, write, start, table, terms, total)
    put(start)
    filtered(read_end, write, end, table, terms, total)
    put(end)
    if second:
        for s in range(FOLD):
            for level in range(2):
                for p in range(2):
                    for j in range(HALF):
                        send[s, 2 * (1 - r) + level, p, j] = earlier[s, level, p, j]


def sums_kernel(recv, sums):
    for lv in range(2):
        for tile in range(2 * HALF):
            h, j = tile // HALF, tile % HALF
            corr = illum = None
            for f in range(2):
                d = [recv[2 * h + f, lv, p, j] for p in range(2)]
                u = [recv[2 * h + f, 2 + lv, p, j] for p in range(2)]
                one, two = d[0] * u[0] + d[1] * u[1], d[0] * d[0] + d[1] * d[1]
                corr = one if corr is None else corr + one
                illum = two if illum is None else illum + two
            sums[tile // 2, 0, lv, tile % 2] = corr
            sums[tile // 2, 1, lv, tile % 2] = illum


def unpack_kernel(recv, down, up):
    for n, out in enumerate((down, up)):
        for lv in range(2):
            for p in range(2):
                for tile in range(2 * HALF):
                    for f in range(2):
                        out[lv, p, f, :, columns(tile)] = recv[2 * (tile // HALF) + f, 2 * n + lv, p, tile % HALF]


def image_kernel(recv, image):
    for lv in range(2):
        for t in range(2):
            corr = (recv[0, 0, lv, t] + recv[1, 0, lv, t]) + (recv[2, 0, lv, t] + recv[3, 0, lv, t])
            illum = (recv[0, 1, lv, t] + recv[1, 1, lv, t]) + (recv[2, 1, lv, t] + recv[3, 1, lv, t])
            image[lv, :, columns(t)] = corr / (1.0 + illum)


def local(down_state, up_state, reflect, layer_mask, classes, coeffs):
    depths = lax.axis_size("depth")
    position = lax.axis_index("depth")
    strip = lax.axis_index("strip")
    info = jnp.stack([position % 2, strip % 2, strip // 2]).astype(jnp.int32)
    pairs = [(i, i ^ 1) for i in range(depths)]
    far = [q for i in range(1, depths - 1, 2) for q in ((i, i + 1), (i + 1, i))]
    lookup = jnp.pad(jnp.transpose(coeffs, (2, 1, 3, 0)), ((0, 0), (0, 0), (0, 0), (0, LANES - CLASSES)))
    sources = (down_state, up_state, reflect, layer_mask, classes)
    held = [pltpu.VMEM(a.shape, a.dtype) for a in (jax.ShapeDtypeStruct((2,) + up_state.shape, jnp.float32),) + sources[2:]]
    send = call(
        pack_kernel, (FOLD, HALF * VALUES + VALUES // PACK) + TILE,
        held + [pltpu.SemaphoreType.DMA((5,))], 60 * 1024 * 1024, info, *sources, stay=5,
    )
    recv = lax.all_to_all(send, "strip", 0, 0)
    folded = (2, WIDE, FOLD) + TILE
    end1, start1, end2, start2, coupling, cells = call(
        fold_kernel, [FIELD] * 4 + [folded] * 2, [(VALUES, WIDE, FOLD * ROWS, LANES)], 16 << 20, info, recv
    )
    from_far = lax.ppermute(end1, "depth", far)
    from_core = lax.ppermute(end2, "depth", pairs)
    table = call(table_kernel, (2, TERMS) + FIELD, [], 16 << 20, info, cells, lookup)
    work = [(3,) + FIELD, FIELD]

    def first(second, entry, other, *after):
        body = functools.partial(first_kernel, second)
        return call(body, [FIELD, FIELD], work, 16 << 20, info, entry, *other, coupling, table, *after)

    def last(second, entry, other, *earlier):
        body = functools.partial(second_kernel, second)
        out = (FOLD, 4 if second else 2, 2, HALF) + TILE
        scratch = [FIELD, (2, WIDE, FOLD * ROWS, LANES)] + work
        return call(body, out, scratch, 16 << 20, info, entry, *other, coupling, table, *earlier)

    one = first(False, from_core, (start2, end2))
    ahead = lax.ppermute(one[1], "depth", far)
    two = first(True, from_far, (start1, end1), one[0])
    from_core = lax.ppermute(two[1], "depth", pairs)
    part = last(False, from_core, two)
    send = last(True, ahead, one, part)
    recv = lax.all_to_all(send, "strip", 0, 0)
    sums = call(sums_kernel, (4, 2, 2, 2) + TILE, [], 16 << 20, recv)
    sums = lax.all_to_all(sums, "freq", 0, 0)
    down, up = call(unpack_kernel, [down_state.shape, up_state.shape], [], 16 << 20, recv)
    image = call(image_kernel, (2, ROWS, 2 * LANES), [], 4 << 20, sums)
    return down, up, image


def solution(mesh):
    placed = (
        P("depth", None, "freq", "strip", None),
        P("depth", None, "freq", "strip", None),
        P("depth", "strip", None),
        P("depth", "strip", None),
        P("depth", "strip", None),
        P(None, None, "freq", None),
    )
    return jax.shard_map(
        local,
        mesh=mesh,
        in_specs=placed,
        out_specs=(
            P("depth", None, "freq", "strip", None),
            P("depth", None, "freq", "strip", None),
            P("depth", "strip", "freq"),
        ),
        check_vma=False,
    )
```

```python
import functools

import jax
import jax.numpy as jnp
from jax import lax
from jax.experimental import pallas as pl
from jax.experimental.pallas import tpu as pltpu
from jax.sharding import PartitionSpec as P


TERMS = 8
CLASSES = 64
LANES = 128
ROWS = 8
WIDE = 5
HALF = 4
FOLD = 4
EDGE = 32
PACK = LANES // EDGE
FIRST = 4 * HALF + 1
TILE = (ROWS, LANES)
FIELD = (2, WIDE, FOLD) + TILE

VM = pl.BlockSpec(memory_space=pltpu.VMEM)
HB = pl.BlockSpec(memory_space=pltpu.HBM)


def call(body, outs, scratch, limit, *args, stay=0):
    many = isinstance(outs, (list, tuple)) and isinstance(outs[0], (list, tuple))
    shapes = [jax.ShapeDtypeStruct(s, jnp.float32) for s in outs] if many else jax.ShapeDtypeStruct(outs, jnp.float32)
    return pl.pallas_call(
        body,
        out_shape=shapes,
        in_specs=[HB if n < stay else VM for n in range(len(args))],
        out_specs=[VM] * len(outs) if many else VM,
        scratch_shapes=[pltpu.VMEM(s, jnp.float32) if isinstance(s, tuple) else s for s in scratch],
        compiler_params=pltpu.CompilerParams(vmem_limit_bytes=limit),
    )(*args)


def columns(tile):
    return slice(tile * LANES, (tile + 1) * LANES)


def pack_kernel(*refs):
    down, up, reflect, mask, classes, *turns, send2, fields, reflects, masks, cells, sems, send1 = refs
    held = (fields.at[0], fields.at[1], reflects, masks, cells)
    copies = [pltpu.make_async_copy(a, b, sems.at[n]) for n, (a, b) in enumerate(zip(refs[:5], held))]
    for copy in copies:
        copy.start()
    for copy in copies:
        copy.wait()
    parity = lax.axis_index("depth") % 2
    lane = lax.broadcasted_iota(jnp.int32, TILE, 1)
    for tile in range(2 * HALF):
        at = columns(tile)
        shared = [reflects[lv, :, at] * masks[lv, :, at].astype(jnp.float32) for lv in range(2)]
        shared += [cells[lv, :, at].astype(jnp.float32) for lv in range(2)]
        h = tile // HALF
        for f in range(2):
            for r, more, send in ((1 - parity, [], send1), (parity, shared, send2)):
                values = [fields[r, level, p, f, :, at] for level in (1 - r, r) for p in range(2)] + more
                for v, value in enumerate(values):
                    send[2 * h + f, HALF * v + tile % HALF] = value
                if tile not in (HALF - 1, HALF):
                    continue
                from_lane = 0 if tile == HALF else LANES - EDGE
                for group in range(len(values) // PACK):
                    packed = None
                    for q in range(PACK):
                        shift = (EDGE * q - from_lane) % LANES
                        moved = values[PACK * group + q]
                        moved = pltpu.roll(moved, shift, 1) if shift else moved
                        packed = moved if packed is None else jnp.where(lane >= EDGE * q, moved, packed)
                    send[2 * (1 - h) + f, HALF * len(values) + group] = packed
    here = lax.axis_index("strip")
    for turn, out in enumerate(turns):
        out[...] = send1[lax.rem(here + turn, FOLD)]


def fold_kernel(sources, *refs):
    recv, outs, rows = refs[:sources], refs[sources:-1], refs[-1]
    values = 2 * len(outs)
    here = lax.axis_index("strip")
    h = here // 2
    lane = lax.broadcasted_iota(jnp.int32, TILE, 1)
    inside = jnp.where(h == 0, lane, LANES - 1 - lane) < EDGE
    for n in range(FOLD):
        if sources == 1:
            block, s = recv[0].at[n], n
        else:
            block, s = recv[n], lax.rem(here + FOLD - n, FOLD)
        at = pl.ds(pl.multiple_of(s * ROWS, ROWS), ROWS)
        for v in range(values):
            for j in range(HALF):
                rows[v, h + j, at, :] = block[HALF * v + j]
            packed = block[HALF * values + v // PACK]
            moved = pltpu.roll(packed, (LANES - EDGE * (v % PACK)) % LANES + (LANES - EDGE) * h, 1)
            rows[v, HALF * (1 - h), at, :] = jnp.where(inside, moved, 0.0)
    for n, out in enumerate(outs):
        for j in range(WIDE):
            for i in range(FOLD):
                for p in range(2):
                    out[p, j, i] = rows[2 * n + p, j, pl.ds(i, ROWS, stride=FOLD), :]


def table_kernel(cells, coeffs, table):
    f = lax.axis_index("strip") % 2
    spots = [(order, p) for order in range(TERMS) for p in range(2)]
    lookups = [jnp.broadcast_to(coeffs[f, p, order : order + 1, :], TILE) for order, p in spots]

    def build(j, carry):
        for lv in range(2):
            for i in range(FOLD):
                cls = cells[lv, j, i].astype(jnp.int32)
                for (order, p), lookup in zip(spots, lookups):
                    table[lv, order, p, j, i] = jnp.take_along_axis(lookup, cls, axis=1, mode="promise_in_bounds")
        return carry

    lax.fori_loop(0, WIDE, build, 0)


def filtered(read, write, level, table, terms, total):
    lane = lax.broadcasted_iota(jnp.int32, TILE, 1)
    sub = lax.broadcasted_iota(jnp.int32, TILE, 0)
    first_lane, last_lane = lane == 0, lane == LANES - 1
    first_sub, last_sub = sub == 0, sub == ROWS - 1
    spots = [(i, j) for i in range(FOLD) for j in range(WIDE)]

    def gather(order, i, j, real, imag):
        cr, ci = table[level, order, 0, j, i], table[level, order, 1, j, i]
        return cr * real - ci * imag, cr * imag + ci * real

    for i, j in spots:
        real, imag = read(0, j, i), read(1, j, i)
        terms[0, 0, j, i], terms[0, 1, j, i] = real, imag
        total[0, j, i], total[1, j, i] = gather(0, i, j, real, imag)
    for order in range(1, TERMS):
        now, before, new = (order - 1) % 3, (order - 2) % 3, order % 3
        for i in range(FOLD):
            made = []
            for p in range(2):
                here = [terms[now, p, j, i] for j in range(WIDE)]
                ahead = [pltpu.roll(x, 1, 1) for x in here]
                behind = [pltpu.roll(x, LANES - 1, 1) for x in here]
                row = []
                for j in range(WIDE):
                    west = jnp.where(first_lane, ahead[j - 1] if j else 0.0, ahead[j])
                    east = jnp.where(last_lane, behind[j + 1] if j + 1 < WIDE else 0.0, behind[j])
                    if i:
                        north = terms[now, p, j, i - 1]
                    else:
                        north = jnp.where(first_sub, 0.0, pltpu.roll(terms[now, p, j, FOLD - 1], 1, 0))
                    if i + 1 < FOLD:
                        south = terms[now, p, j, i + 1]
                    else:
                        south = jnp.where(last_sub, 0.0, pltpu.roll(terms[now, p, j, 0], ROWS - 1, 0))
                    around = (south + north) + (east + west)
                    if order == 1:
                        term = around * 0.25
                    else:
                        term = around * 0.5 - terms[before, p, j, i]
                    row.append(term)
                    if order + 1 < TERMS:
                        terms[new, p, j, i] = term
                made.append(row)
            for j in range(WIDE):
                dr, di = gather(order, i, j, made[0][j], made[1][j])
                real, imag = total[0, j, i] + dr, total[1, j, i] + di
                if order + 1 < TERMS:
                    total[0, j, i], total[1, j, i] = real, imag
                else:
                    write(0, j, i, real)
                    write(1, j, i, imag)


def direction(second):
    parity = lax.axis_index("depth") % 2
    return parity if second else 1 - parity


def first_kernel(second, entry, start_other, end_other, coupling, table, *refs):
    start_out, end_out, terms, total = refs[-4:]
    r = direction(second)
    start, end = r, 1 - r

    def read_start(p, j, i):
        return entry[p, j, i] + coupling[start, j, i] * end_other[p, j, i]

    def read_end(p, j, i):
        return start_out[p, j, i] + coupling[end, j, i] * start_other[p, j, i]

    def write_start(p, j, i, x):
        start_out[p, j, i] = x

    def write_end(p, j, i, x):
        end_out[p, j, i] = x

    filtered(read_start, write_start, start, table, terms, total)
    filtered(read_end, write_end, end, table, terms, total)


def second_kernel(second, entry, start_other, end_other, coupling, table, *refs):
    if second:
        earlier, send, result, rows, terms, total = refs
    else:
        send, result, rows, terms, total = refs
    r, h = direction(second), lax.axis_index("strip") // 2
    start, end = r, 1 - r

    def read_start(p, j, i):
        return entry[p, j, i] + coupling[start, j, i] * end_other[p, j, i]

    def read_end(p, j, i):
        return result[p, j, i] + coupling[end, j, i] * start_other[p, j, i]

    def write(p, j, i, x):
        result[p, j, i] = x
        rows[p, j, pl.ds(i, ROWS, stride=FOLD), :] = x

    def put(level):
        for p in range(2):
            for j in range(HALF):
                for s in range(FOLD):
                    value = rows[p, h + j, s * ROWS : (s + 1) * ROWS, :]
                    if second:
                        send[s, 2 * r + level, p, j] = value
                    else:
                        send[s, level, p, j] = value

    filtered(read_start, write, start, table, terms, total)
    put(start)
    filtered(read_end, write, end, table, terms, total)
    put(end)
    if second:
        for s in range(FOLD):
            for level in range(2):
                for p in range(2):
                    for j in range(HALF):
                        send[s, 2 * (1 - r) + level, p, j] = earlier[s, level, p, j]


def sums_kernel(recv, sums):
    for lv in range(2):
        for tile in range(2 * HALF):
            h, j = tile // HALF, tile % HALF
            corr = illum = None
            for f in range(2):
                d = [recv[2 * h + f, lv, p, j] for p in range(2)]
                u = [recv[2 * h + f, 2 + lv, p, j] for p in range(2)]
                one, two = d[0] * u[0] + d[1] * u[1], d[0] * d[0] + d[1] * d[1]
                corr = one if corr is None else corr + one
                illum = two if illum is None else illum + two
            sums[tile // 2, 0, lv, tile % 2] = corr
            sums[tile // 2, 1, lv, tile % 2] = illum


def unpack_kernel(recv, down, up):
    for n, out in enumerate((down, up)):
        for lv in range(2):
            for p in range(2):
                for tile in range(2 * HALF):
                    for f in range(2):
                        out[lv, p, f, :, columns(tile)] = recv[2 * (tile // HALF) + f, 2 * n + lv, p, tile % HALF]


def copy_kernel(source, target):
    target[...] = source[...]


def image_kernel(recv, image):
    for lv in range(2):
        for t in range(2):
            corr = (recv[0, 0, lv, t] + recv[1, 0, lv, t]) + (recv[2, 0, lv, t] + recv[3, 0, lv, t])
            illum = (recv[0, 1, lv, t] + recv[1, 1, lv, t]) + (recv[2, 1, lv, t] + recv[3, 1, lv, t])
            image[lv, :, columns(t)] = corr / (1.0 + illum)


def local(down_state, up_state, reflect, layer_mask, classes, coeffs):
    depths = lax.axis_size("depth")
    pairs = [(i, i ^ 1) for i in range(depths)]
    far = [q for i in range(1, depths - 1, 2) for q in ((i, i + 1), (i + 1, i))]
    lookup = jnp.pad(jnp.transpose(coeffs, (2, 1, 3, 0)), ((0, 0), (0, 0), (0, 0), (0, LANES - CLASSES)))
    sources = (down_state, up_state, reflect, layer_mask, classes)
    held = [pltpu.VMEM(a.shape, a.dtype) for a in (jax.ShapeDtypeStruct((2,) + up_state.shape, jnp.float32),) + sources[2:]]
    *turns, send2 = call(
        pack_kernel, [(FIRST,) + TILE] * FOLD + [(FOLD, 2 * FIRST) + TILE],
        held + [pltpu.SemaphoreType.DMA((5,)), (FOLD, FIRST) + TILE], 60 * 1024 * 1024, *sources, stay=5,
    )
    strips = range(lax.axis_size("strip"))
    for turn in range(1, FOLD):
        turns[turn] = lax.ppermute(turns[turn], "strip", [(s, (s + turn) % FOLD) for s in strips])
    recv2 = lax.all_to_all(send2, "strip", 0, 0)
    folded = (2, WIDE, FOLD) + TILE
    rows = (WIDE, FOLD * ROWS, LANES)
    end1, start1 = call(functools.partial(fold_kernel, 4), [FIELD] * 2, [(4,) + rows], 16 << 20, *turns)
    from_far = lax.ppermute(end1, "depth", far)
    lookup = call(copy_kernel, lookup.shape, [], 4 << 20, lookup)
    end2, start2, coupling, cells = call(
        functools.partial(fold_kernel, 1), [FIELD] * 2 + [folded] * 2, [(8,) + rows], 16 << 20, recv2
    )
    from_core = lax.ppermute(end2, "depth", pairs)
    table = call(table_kernel, (2, TERMS) + FIELD, [], 16 << 20, cells, lookup)
    work = [(3,) + FIELD, FIELD]

    def first(second, entry, other, *after):
        body = functools.partial(first_kernel, second)
        return call(body, [FIELD, FIELD], work, 16 << 20, entry, *other, coupling, table, *after)

    def last(second, entry, other, *earlier):
        body = functools.partial(second_kernel, second)
        out = (FOLD, 4 if second else 2, 2, HALF) + TILE
        return call(body, out, [FIELD, (2,) + rows] + work, 16 << 20, entry, *other, coupling, table, *earlier)

    one = first(False, from_core, (start2, end2))
    ahead = lax.ppermute(one[1], "depth", far)
    two = first(True, from_far, (start1, end1), one[0])
    from_core = lax.ppermute(two[1], "depth", pairs)
    part = last(False, from_core, two)
    send = last(True, ahead, one, part)
    recv = lax.all_to_all(send, "strip", 0, 0)
    sums = call(sums_kernel, (4, 2, 2, 2) + TILE, [], 16 << 20, recv)
    sums = lax.all_to_all(sums, "freq", 0, 0)
    down, up = call(unpack_kernel, [down_state.shape, up_state.shape], [], 16 << 20, recv)
    image = call(image_kernel, (2, ROWS, 2 * LANES), [], 4 << 20, sums)
    return down, up, image


def solution(mesh):
    placed = (
        P("depth", None, "freq", "strip", None),
        P("depth", None, "freq", "strip", None),
        P("depth", "strip", None),
        P("depth", "strip", None),
        P("depth", "strip", None),
        P(None, None, "freq", None),
    )
    return jax.shard_map(
        local,
        mesh=mesh,
        in_specs=placed,
        out_specs=(
            P("depth", None, "freq", "strip", None),
            P("depth", None, "freq", "strip", None),
            P("depth", "strip", "freq"),
        ),
        check_vma=False,
    )
```

```python
import functools

import jax
import jax.numpy as jnp
from jax import lax
from jax.experimental import pallas as pl
from jax.experimental.pallas import tpu as pltpu
from jax.sharding import PartitionSpec as P


TERMS = 8
CLASSES = 64
LANES = 128
ROWS = 8
WIDE = 5
HALF = 4
FOLD = 4
EDGE = 32
PACK = LANES // EDGE
FIRST = 4 * HALF + 1
TILE = (ROWS, LANES)
FIELD = (2, WIDE, FOLD) + TILE
MESSAGE = (2 * HALF * FOLD + 2,) + TILE

VM = pl.BlockSpec(memory_space=pltpu.VMEM)
HB = pl.BlockSpec(memory_space=pltpu.HBM)


def call(body, outs, scratch, limit, *args, stay=0):
    many = isinstance(outs, (list, tuple)) and isinstance(outs[0], (list, tuple))
    shapes = [jax.ShapeDtypeStruct(s, jnp.float32) for s in outs] if many else jax.ShapeDtypeStruct(outs, jnp.float32)
    return pl.pallas_call(
        body,
        out_shape=shapes,
        in_specs=[HB if n < stay else VM for n in range(len(args))],
        out_specs=[VM] * len(outs) if many else VM,
        scratch_shapes=[pltpu.VMEM(s, jnp.float32) if isinstance(s, tuple) else s for s in scratch],
        compiler_params=pltpu.CompilerParams(vmem_limit_bytes=limit),
    )(*args)


def columns(tile):
    return slice(tile * LANES, (tile + 1) * LANES)


def pack_kernel(*refs):
    down, up, reflect, mask, classes, *turns, send2, fields, reflects, masks, cells, sems, send1 = refs
    held = (fields.at[0], fields.at[1], reflects, masks, cells)
    copies = [pltpu.make_async_copy(a, b, sems.at[n]) for n, (a, b) in enumerate(zip(refs[:5], held))]
    for copy in copies:
        copy.start()
    for copy in copies:
        copy.wait()
    parity = lax.axis_index("depth") % 2
    lane = lax.broadcasted_iota(jnp.int32, TILE, 1)
    for tile in range(2 * HALF):
        at = columns(tile)
        shared = [reflects[lv, :, at] * masks[lv, :, at].astype(jnp.float32) for lv in range(2)]
        shared += [cells[lv, :, at].astype(jnp.float32) for lv in range(2)]
        h = tile // HALF
        for f in range(2):
            for r, more, send in ((1 - parity, [], send1), (parity, shared, send2)):
                values = [fields[r, level, p, f, :, at] for level in (1 - r, r) for p in range(2)] + more
                for v, value in enumerate(values):
                    send[2 * h + f, HALF * v + tile % HALF] = value
                if tile not in (HALF - 1, HALF):
                    continue
                from_lane = 0 if tile == HALF else LANES - EDGE
                for group in range(len(values) // PACK):
                    packed = None
                    for q in range(PACK):
                        shift = (EDGE * q - from_lane) % LANES
                        moved = values[PACK * group + q]
                        moved = pltpu.roll(moved, shift, 1) if shift else moved
                        packed = moved if packed is None else jnp.where(lane >= EDGE * q, moved, packed)
                    send[2 * (1 - h) + f, HALF * len(values) + group] = packed
    here = lax.axis_index("strip")
    for turn, out in enumerate(turns):
        out[...] = send1[lax.rem(here + turn, FOLD)]


def halo_of(packed, q, h):
    lane = lax.broadcasted_iota(jnp.int32, TILE, 1)
    inside = jnp.where(h == 0, lane, LANES - 1 - lane) < EDGE
    moved = pltpu.roll(packed, (LANES - EDGE * q) % LANES + (LANES - EDGE) * h, 1)
    return jnp.where(inside, moved, 0.0)


def put_message(message, field):
    h = lax.axis_index("strip") // 2
    lane = lax.broadcasted_iota(jnp.int32, TILE, 1)
    for p in range(2):
        packed = None
        for i in range(FOLD):
            for j in range(HALF):
                message[(p * HALF + j) * FOLD + i] = field[p, h + j, i]
            moved = pltpu.roll(field[p, HALF * (1 - h), i], EDGE * (i + h), 1)
            packed = moved if packed is None else jnp.where(lane >= EDGE * i, moved, packed)
        message[2 * HALF * FOLD + p] = packed


def take_message(message, field):
    h = lax.axis_index("strip") // 2
    for p in range(2):
        for i in range(FOLD):
            for j in range(HALF):
                field[p, h + j, i] = message[(p * HALF + j) * FOLD + i]
            field[p, HALF * (1 - h), i] = halo_of(message[2 * HALF * FOLD + p], i, h)


def fold_kernel(sources, *refs):
    recv, outs, rows = refs[:sources], refs[sources:-1], refs[-1]
    if sources > 1:
        outs, message = outs[:-1], outs[-1]
    values = 2 * len(outs)
    here = lax.axis_index("strip")
    h = here // 2
    for n in range(FOLD):
        if sources == 1:
            block, s = recv[0].at[n], n
        else:
            block, s = recv[n], lax.rem(here + FOLD - n, FOLD)
        at = pl.ds(pl.multiple_of(s * ROWS, ROWS), ROWS)
        for v in range(values):
            for j in range(HALF):
                rows[v, h + j, at, :] = block[HALF * v + j]
            rows[v, HALF * (1 - h), at, :] = halo_of(block[HALF * values + v // PACK], v % PACK, h)
    for n, out in enumerate(outs):
        for j in range(WIDE):
            for i in range(FOLD):
                for p in range(2):
                    out[p, j, i] = rows[2 * n + p, j, pl.ds(i, ROWS, stride=FOLD), :]
    if sources > 1:
        put_message(message, outs[0])


def table_kernel(cells, coeffs, table):
    f = lax.axis_index("strip") % 2
    spots = [(order, p) for order in range(TERMS) for p in range(2)]
    lookups = [jnp.broadcast_to(coeffs[f, p, order : order + 1, :], TILE) for order, p in spots]

    def build(j, carry):
        for lv in range(2):
            for i in range(FOLD):
                cls = cells[lv, j, i].astype(jnp.int32)
                for (order, p), lookup in zip(spots, lookups):
                    table[lv, order, p, j, i] = jnp.take_along_axis(lookup, cls, axis=1, mode="promise_in_bounds")
        return carry

    lax.fori_loop(0, WIDE, build, 0)


def filtered(read, write, level, table, terms, total):
    lane = lax.broadcasted_iota(jnp.int32, TILE, 1)
    sub = lax.broadcasted_iota(jnp.int32, TILE, 0)
    first_lane, last_lane = lane == 0, lane == LANES - 1
    first_sub, last_sub = sub == 0, sub == ROWS - 1
    spots = [(i, j) for i in range(FOLD) for j in range(WIDE)]

    def gather(order, i, j, real, imag):
        cr, ci = table[level, order, 0, j, i], table[level, order, 1, j, i]
        return cr * real - ci * imag, cr * imag + ci * real

    for i, j in spots:
        real, imag = read(0, j, i), read(1, j, i)
        terms[0, 0, j, i], terms[0, 1, j, i] = real, imag
        total[0, j, i], total[1, j, i] = gather(0, i, j, real, imag)
    for order in range(1, TERMS):
        now, before, new = (order - 1) % 3, (order - 2) % 3, order % 3
        for i in range(FOLD):
            made = []
            for p in range(2):
                here = [terms[now, p, j, i] for j in range(WIDE)]
                ahead = [pltpu.roll(x, 1, 1) for x in here]
                behind = [pltpu.roll(x, LANES - 1, 1) for x in here]
                row = []
                for j in range(WIDE):
                    west = jnp.where(first_lane, ahead[j - 1] if j else 0.0, ahead[j])
                    east = jnp.where(last_lane, behind[j + 1] if j + 1 < WIDE else 0.0, behind[j])
                    if i:
                        north = terms[now, p, j, i - 1]
                    else:
                        north = jnp.where(first_sub, 0.0, pltpu.roll(terms[now, p, j, FOLD - 1], 1, 0))
                    if i + 1 < FOLD:
                        south = terms[now, p, j, i + 1]
                    else:
                        south = jnp.where(last_sub, 0.0, pltpu.roll(terms[now, p, j, 0], ROWS - 1, 0))
                    around = (south + north) + (east + west)
                    if order == 1:
                        term = around * 0.25
                    else:
                        term = around * 0.5 - terms[before, p, j, i]
                    row.append(term)
                    if order + 1 < TERMS:
                        terms[new, p, j, i] = term
                made.append(row)
            for j in range(WIDE):
                dr, di = gather(order, i, j, made[0][j], made[1][j])
                real, imag = total[0, j, i] + dr, total[1, j, i] + di
                if order + 1 < TERMS:
                    total[0, j, i], total[1, j, i] = real, imag
                else:
                    write(0, j, i, real)
                    write(1, j, i, imag)


def direction(second):
    parity = lax.axis_index("depth") % 2
    return parity if second else 1 - parity


def first_kernel(second, entry, start_other, end_other, coupling, table, *refs):
    if second:
        start_out, end_out, field, terms, total = refs[-5:]
        take_message(entry, field)
        entry = field
    else:
        start_out, end_out, message, terms, total = refs[-5:]
    r = direction(second)
    start, end = r, 1 - r

    def read_start(p, j, i):
        return entry[p, j, i] + coupling[start, j, i] * end_other[p, j, i]

    def read_end(p, j, i):
        return start_out[p, j, i] + coupling[end, j, i] * start_other[p, j, i]

    def write_start(p, j, i, x):
        start_out[p, j, i] = x

    def write_end(p, j, i, x):
        end_out[p, j, i] = x

    filtered(read_start, write_start, start, table, terms, total)
    filtered(read_end, write_end, end, table, terms, total)
    if not second:
        put_message(message, end_out)


def second_kernel(second, entry, start_other, end_other, coupling, table, *refs):
    if second:
        earlier, send, field, result, rows, terms, total = refs
        take_message(entry, field)
        entry = field
    else:
        send, result, rows, terms, total = refs
    r, h = direction(second), lax.axis_index("strip") // 2
    start, end = r, 1 - r

    def read_start(p, j, i):
        return entry[p, j, i] + coupling[start, j, i] * end_other[p, j, i]

    def read_end(p, j, i):
        return result[p, j, i] + coupling[end, j, i] * start_other[p, j, i]

    def write(p, j, i, x):
        result[p, j, i] = x
        rows[p, j, pl.ds(i, ROWS, stride=FOLD), :] = x

    def put(level):
        for p in range(2):
            for j in range(HALF):
                for s in range(FOLD):
                    value = rows[p, h + j, s * ROWS : (s + 1) * ROWS, :]
                    if second:
                        send[s, 2 * r + level, p, j] = value
                    else:
                        send[s, level, p, j] = value

    filtered(read_start, write, start, table, terms, total)
    put(start)
    filtered(read_end, write, end, table, terms, total)
    put(end)
    if second:
        for s in range(FOLD):
            for level in range(2):
                for p in range(2):
                    for j in range(HALF):
                        send[s, 2 * (1 - r) + level, p, j] = earlier[s, level, p, j]


def sums_kernel(recv, sums):
    for lv in range(2):
        for tile in range(2 * HALF):
            h, j = tile // HALF, tile % HALF
            corr = illum = None
            for f in range(2):
                d = [recv[2 * h + f, lv, p, j] for p in range(2)]
                u = [recv[2 * h + f, 2 + lv, p, j] for p in range(2)]
                one, two = d[0] * u[0] + d[1] * u[1], d[0] * d[0] + d[1] * d[1]
                corr = one if corr is None else corr + one
                illum = two if illum is None else illum + two
            sums[tile // 2, 0, lv, tile % 2] = corr
            sums[tile // 2, 1, lv, tile % 2] = illum


def unpack_kernel(recv, down, up):
    for n, out in enumerate((down, up)):
        for lv in range(2):
            for p in range(2):
                for tile in range(2 * HALF):
                    for f in range(2):
                        out[lv, p, f, :, columns(tile)] = recv[2 * (tile // HALF) + f, 2 * n + lv, p, tile % HALF]


def copy_kernel(source, target):
    target[...] = source[...]


def image_kernel(recv, image):
    for lv in range(2):
        for t in range(2):
            corr = (recv[0, 0, lv, t] + recv[1, 0, lv, t]) + (recv[2, 0, lv, t] + recv[3, 0, lv, t])
            illum = (recv[0, 1, lv, t] + recv[1, 1, lv, t]) + (recv[2, 1, lv, t] + recv[3, 1, lv, t])
            image[lv, :, columns(t)] = corr / (1.0 + illum)


def local(down_state, up_state, reflect, layer_mask, classes, coeffs):
    depths = lax.axis_size("depth")
    pairs = [(i, i ^ 1) for i in range(depths)]
    far = [q for i in range(1, depths - 1, 2) for q in ((i, i + 1), (i + 1, i))]
    lookup = jnp.pad(jnp.transpose(coeffs, (2, 1, 3, 0)), ((0, 0), (0, 0), (0, 0), (0, LANES - CLASSES)))
    sources = (down_state, up_state, reflect, layer_mask, classes)
    held = [pltpu.VMEM(a.shape, a.dtype) for a in (jax.ShapeDtypeStruct((2,) + up_state.shape, jnp.float32),) + sources[2:]]
    *turns, send2 = call(
        pack_kernel, [(FIRST,) + TILE] * FOLD + [(FOLD, 2 * FIRST) + TILE],
        held + [pltpu.SemaphoreType.DMA((5,)), (FOLD, FIRST) + TILE], 60 * 1024 * 1024, *sources, stay=5,
    )
    strips = range(lax.axis_size("strip"))
    for turn in range(1, FOLD):
        turns[turn] = lax.ppermute(turns[turn], "strip", [(s, (s + turn) % FOLD) for s in strips])
    recv2 = lax.all_to_all(send2, "strip", 0, 0)
    folded = (2, WIDE, FOLD) + TILE
    rows = (WIDE, FOLD * ROWS, LANES)
    end1, start1, message = call(
        functools.partial(fold_kernel, 4), [FIELD] * 2 + [MESSAGE], [(4,) + rows], 16 << 20, *turns
    )
    from_far = lax.ppermute(message, "depth", far)
    lookup = call(copy_kernel, lookup.shape, [], 4 << 20, lookup)
    end2, start2, coupling, cells = call(
        functools.partial(fold_kernel, 1), [FIELD] * 2 + [folded] * 2, [(8,) + rows], 16 << 20, recv2
    )
    from_core = lax.ppermute(end2, "depth", pairs)
    table = call(table_kernel, (2, TERMS) + FIELD, [], 16 << 20, cells, lookup)
    work = [(3,) + FIELD, FIELD]

    def first(second, entry, other, *after):
        body = functools.partial(first_kernel, second)
        outs, scratch = ([FIELD] * 2, [FIELD] + work) if second else ([FIELD] * 2 + [MESSAGE], work)
        return call(body, outs, scratch, 16 << 20, entry, *other, coupling, table, *after)

    def last(second, entry, other, *earlier):
        body = functools.partial(second_kernel, second)
        out = (FOLD, 4 if second else 2, 2, HALF) + TILE
        scratch = [FIELD] * (2 if second else 1) + [(2,) + rows] + work
        return call(body, out, scratch, 16 << 20, entry, *other, coupling, table, *earlier)

    one = first(False, from_core, (start2, end2))
    ahead = lax.ppermute(one[2], "depth", far)
    two = first(True, from_far, (start1, end1), one[0])
    from_core = lax.ppermute(two[1], "depth", pairs)
    part = last(False, from_core, two)
    send = last(True, ahead, one[:2], part)
    recv = lax.all_to_all(send, "strip", 0, 0)
    sums = call(sums_kernel, (4, 2, 2, 2) + TILE, [], 16 << 20, recv)
    sums = lax.all_to_all(sums, "freq", 0, 0)
    down, up = call(unpack_kernel, [down_state.shape, up_state.shape], [], 16 << 20, recv)
    image = call(image_kernel, (2, ROWS, 2 * LANES), [], 4 << 20, sums)
    return down, up, image


def solution(mesh):
    placed = (
        P("depth", None, "freq", "strip", None),
        P("depth", None, "freq", "strip", None),
        P("depth", "strip", None),
        P("depth", "strip", None),
        P("depth", "strip", None),
        P(None, None, "freq", None),
    )
    return jax.shard_map(
        local,
        mesh=mesh,
        in_specs=placed,
        out_specs=(
            P("depth", None, "freq", "strip", None),
            P("depth", None, "freq", "strip", None),
            P("depth", "strip", "freq"),
        ),
        check_vma=False,
    )
```
